32 devices in a mesh: vblk: 8 (over y, x, core), pair: 4 (over z).
Axes of the slice: x: 2, y: 2, z: 4, core: 2. Of those that a mesh axis runs over, the one named last changes fastest.
Arguments:
- amplitudes: bfloat16 [128, 384, 384], P(('vblk', 'pair')), may hold values from -6 to 6
- domain_mask: int32 [128, 3], P(('vblk', 'pair')), may hold values from 0 to 1, as said below
- centers: int32 [128], P(('vblk', 'pair')), may hold values from 0 to 7, as said below
- chol_panel: bfloat16 [8, 8, 5, 128, 128], P('vblk', None, None, 'pair'), may hold values from -0.3125 to 0.3125
Outputs:
- residual_tiles: float32 [128, 384, 384], P(('vblk', 'pair'))
The draws below stay inside these ranges and needn't reach their ends.
Inputs may be any that keep to these rules, and one draw needn't show every extreme that they name: centers[p] differs from p // 16 (the block of the region that holds pair p) by at most 1, and by exactly 1 in both directions for some pairs. `domain_mask`: the middle column of the window (column 1 for a window of 3 blocks) is 1 for every pair; column k is 0 where the window block centers + k minus the middle index lies outside 0 to 7.
All inputs are finite; a program needn't handle non-finite values.
Results may differ from the reference program's by a relative error of at most 0.0029.
Values may be sent and summed in bfloat16 or wider, within the bound.
No kernel may reach another device: no remote copies, remote signals or barrier semaphores. Data moves between devices by JAX's collectives and lax.ppermute only.
A program may use at most 128 MiB of HBM per device.

```python
import jax
import jax.numpy as jnp
from jax import lax

VB = 128
DW = 3
RCH = 1
NQ = 8
PW = 5
NVB = 8
PAIRS_COL = 16
NPAIR = 128


def pair_layout(key):
    layout_key = jax.random.fold_in(key, 7)
    home = jnp.arange(NPAIR, dtype=jnp.int32) // PAIRS_COL
    stride = jax.random.randint(jax.random.fold_in(layout_key, 1), (NPAIR,), -RCH, RCH + 1).astype(jnp.int32)
    middle = NVB // 2 * PAIRS_COL
    stride = stride.at[middle].set(RCH).at[middle + 1].set(-RCH)
    return jnp.clip(home + stride, 0, NVB - 1).astype(jnp.int32)


def draw_centers(key, part):
    return pair_layout(key)


def draw_domain_mask(key, part):
    centre = pair_layout(key)
    sides = jax.random.randint(jax.random.fold_in(key, 11), (NPAIR, DW), 0, 2).astype(jnp.int32)
    sides = sides.at[:, (DW - 1) // 2].set(1)
    position = centre[:, None] + jnp.arange(DW, dtype=jnp.int32)[None, :] - (DW - 1) // 2
    inside = (position >= 0) & (position < NVB)
    return jnp.where(inside, sides, 0).astype(jnp.int32)


def steps_of(own_key, shape, shards, smallest, top_value):
    factor_of = 1.0
    for dim, parts in shards:
        draws = jax.random.uniform(jax.random.fold_in(jax.random.fold_in(own_key, 6), dim), (parts,), jnp.float32, smallest / len(shards), top_value / len(shards))
        factor_of = factor_of * jnp.repeat(jnp.exp(draws), shape[dim] // parts).reshape((-1,) + (1,) * (len(shape) - 1 - dim))
    return factor_of


def centred(own_key, dims, spread, bound, shards=(), kind=jnp.bfloat16):
    loudness = steps_of(own_key, dims, shards, -0.22, 0.18) if shards else 1.0
    entries = jax.random.normal(own_key, dims, jnp.float32) * spread * loudness
    return jnp.minimum(jnp.maximum(entries, -bound), bound).astype(kind)


def setup_inputs(seed: int = 0) -> dict:
    seeds = jax.random.split(jax.random.key(seed), 5)
    return {
        "amplitudes": centred(seeds[0], (NPAIR, DW * VB, DW * VB), 1.0, 6.0, ((0, 32),)),
        "domain_mask": draw_domain_mask(jax.random.fold_in(seeds[4], 71), 0),
        "centers": draw_centers(jax.random.fold_in(seeds[4], 71), 0),
        "chol_panel": centred(seeds[3], (NVB, NQ, PW, VB, VB), (DW * VB) ** -0.5, 0.3125, ((0, 8), (3, 4))),
    }


def assemble(window):
    strips = []
    for a in range(DW):
        strips.append(jnp.concatenate([window[..., a, :, b - a + DW - 1, :, :] for b in range(DW)], axis=-1))
    return jnp.concatenate(strips, axis=-2)


def reference(amplitudes, domain_mask, centers, chol_panel):
    halfwidth = (DW - 1) // 2

    def single(record):
        amplitude, live_mask, centre = record
        row_index = jnp.clip(centre - halfwidth + jnp.arange(DW, dtype=jnp.int32), 0, NVB - 1).astype(jnp.int32)
        window = jnp.take(chol_panel, row_index, axis=0)
        blocks = assemble(window)
        live_cols = jnp.repeat(live_mask, VB) > 0
        keep_tile = live_cols[:, None] & live_cols[None, :]
        masked = jnp.where(keep_tile, amplitude, jnp.zeros_like(amplitude))
        half_product = jnp.einsum("qij,jk->qik", blocks.astype(jnp.float32), masked.astype(jnp.float32)).astype(jnp.bfloat16)
        ladder = jnp.einsum("qik,qlk->il", half_product.astype(jnp.float32), blocks.astype(jnp.float32))
        return jnp.where(keep_tile, ladder, jnp.zeros_like(ladder))

    return lax.map(single, (amplitudes, domain_mask, centers))
```

```python
import functools

import jax
import jax.numpy as jnp
from jax import lax
from jax.experimental import pallas as pl
from jax.experimental.pallas import tpu as pltpu
from jax.sharding import PartitionSpec as P

VB = 128
DW = 3
CHUNKS = (2, 2, 2, 2)
AXES = ("vblk", "pair")


def ladder_kernel(chunk, has_sum, *refs):
    if has_sum:
        rel_ref, live_ref, where_ref, amp_ref, *panels, sum_ref, out_ref, tiles, strips, halves, sem = refs
    else:
        rel_ref, live_ref, where_ref, amp_ref, *panels, out_ref, tiles, strips, halves, sem = refs
    shards = panels[0].shape[0]
    rows = panels[0].shape[3]
    npair = amp_ref.shape[0]

    def copy(i, s):
        at = where_ref[0, i]
        row = pl.multiple_of(where_ref[1, s] * rows, rows)
        return pltpu.make_async_copy(
            panels[i].at[s], tiles.at[at, :, :, pl.ds(row, rows), :], sem.at[i, s]
        )

    for i in range(len(panels)):
        for s in range(shards):
            copy(i, s).start()
    for i in range(len(panels)):
        for s in range(shards):
            copy(i, s).wait()

    @pl.loop(0, npair)
    def _(p):
        rel = rel_ref[p]
        live = [live_ref[p, k] > 0 for k in range(DW)]
        masked = jnp.concatenate(
            [
                jnp.concatenate(
                    [
                        jnp.where(live[a] & live[b], amp_ref[p, pl.ds(a * VB, VB), pl.ds(b * VB, VB)], 0)
                        for b in range(DW)
                    ],
                    axis=1,
                )
                for a in range(DW)
            ],
            axis=0,
        ).astype(jnp.bfloat16)
        for q in range(chunk):
            for a in range(DW):
                strips[pl.ds(a * VB, VB), pl.ds(q * DW * VB, DW * VB)] = jnp.concatenate(
                    [tiles[rel + a, q, b - a + DW - 1] for b in range(DW)], axis=1
                )
        for q in range(chunk):
            cols = pl.ds(q * DW * VB, DW * VB)
            halves[:, cols] = jnp.dot(
                strips[:, cols], masked, preferred_element_type=jnp.float32
            ).astype(jnp.bfloat16)
        ladder = lax.dot_general(
            halves[...], strips[...], (((1,), (1,)), ((), ())), preferred_element_type=jnp.float32
        )
        for a in range(DW):
            for b in range(DW):
                at = (p, pl.ds(a * VB, VB), pl.ds(b * VB, VB))
                part = ladder[a * VB : (a + 1) * VB, b * VB : (b + 1) * VB]
                if has_sum:
                    part = part + sum_ref[at]
                out_ref[at] = jnp.where(live[a] & live[b], part, 0.0)


def ladder(chunk, rel, live, where, amplitudes, panels, total):
    npair, width, _ = amplitudes.shape
    vmem = pl.BlockSpec(memory_space=pltpu.VMEM)
    smem = pl.BlockSpec(memory_space=pltpu.SMEM)
    anyspace = pl.BlockSpec(memory_space=pl.ANY)
    shards, _, offs, rows, vb = panels[0].shape
    sums = [] if total is None else [total]
    flops = npair * chunk * 4 * width**3
    return pl.pallas_call(
        functools.partial(ladder_kernel, chunk, bool(sums)),
        out_shape=jax.ShapeDtypeStruct((npair, width, width), jnp.float32),
        in_specs=[smem, smem, smem, vmem] + [anyspace] * len(panels) + [vmem] * len(sums),
        out_specs=vmem,
        scratch_shapes=[
            pltpu.VMEM((2 * DW, chunk, offs, shards * rows, vb), jnp.bfloat16),
            pltpu.VMEM((width, chunk * width), jnp.bfloat16),
            pltpu.VMEM((width, chunk * width), jnp.bfloat16),
            pltpu.SemaphoreType.DMA((len(panels), shards)),
        ],
        cost_estimate=pl.CostEstimate(flops=flops, bytes_accessed=6 << 20, transcendentals=0),
    )(rel, live, where, amplitudes, *panels, *sums)


def solution(mesh):
    nv, nz = mesh.shape["vblk"], mesh.shape["pair"]
    chips = nv // 2

    def moves(step):
        pairs = []
        for v in range(nv):
            for z in range(nz):
                to = step(v // 2, v % 2, z)
                if to is not None and 0 <= to[0] < chips:
                    pairs.append((v * nz + z, (to[0] * 2 + to[1]) * nz + to[2]))
        return pairs

    sideways = [moves(lambda i, c, z, s=s: (i, c, z ^ s)) for s in range(1, nz)]
    neighbour = moves(lambda i, c, z: (i ^ 1, c, z))
    relay = moves(lambda i, c, z: (i - 2 if i % 2 else i + 2, c, z))
    sibling = moves(lambda i, c, z: (i, 1 - c, z))

    def local(amplitudes, domain_mask, centers, chol_panel):
        v = lax.axis_index("vblk")
        z = lax.axis_index("pair")
        chip, core = v // 2, v % 2
        odd = chip % 2
        rel = centers - v + 1
        unused = 2 * DW - 1
        near = jnp.where(core == 0, 1, 3)
        use_nb = core != odd
        places = jnp.stack(
            [
                2 + 0 * v,
                jnp.where(odd == 1, 0, 4),
                jnp.where(odd == 1, 4, 0),
                jnp.where(core == 0, 3, 1),
                jnp.where(use_nb, near, unused),
                jnp.where(use_nb, unused, near),
            ]
        )
        slots = z ^ jnp.arange(6, dtype=jnp.int32)
        where = jnp.stack([places, slots]).astype(jnp.int32)
        total = None
        start = 0
        for chunk in CHUNKS:
            own = chol_panel[0, start : start + chunk]
            start += chunk
            gathered = jnp.stack([own] + [lax.ppermute(own, AXES, m) for m in sideways])
            swapped = lax.ppermute(gathered, AXES, neighbour)
            relayed = lax.ppermute(swapped, AXES, relay)
            mine = [gathered, swapped, relayed]
            panels = mine + [lax.ppermute(x, AXES, sibling) for x in mine]
            total = ladder(chunk, rel, domain_mask, where, amplitudes, panels, total)
        return total

    return jax.shard_map(
        local,
        mesh=mesh,
        in_specs=(
            P(AXES, None, None),
            P(AXES, None),
            P(AXES),
            P("vblk", None, None, "pair", None),
        ),
        out_specs=P(AXES, None, None),
        check_vma=False,
    )
```

```python
import functools

import jax
import jax.numpy as jnp
from jax import lax
from jax.experimental import pallas as pl
from jax.experimental.pallas import tpu as pltpu
from jax.sharding import PartitionSpec as P

VB = 128
DW = 3
PANELS = 6
CHUNKS = (1, 1, 1, 1)
KGROUPS = ((0,), (1,), (2,), (3,))
OWN_FIRST = True
DEPS = {'x_3': ['k_0'], 'y_3': ['k_1'], 'z_2': ['x_own']}
AXES = ("vblk", "pair")


def ladder_kernel(plan, chunk, sets, npanel, has_sum, *refs):
    refs = list(refs)
    place_ref = refs.pop(0)
    info_refs = [refs.pop(0) for _ in range(sets)]
    amp_refs = [refs.pop(0) for _ in range(sets)]
    panel_refs = [refs.pop(0) for _ in range(npanel)]
    sum_refs = [refs.pop(0) for _ in range(sets)] if has_sum else []
    out_refs = [refs.pop(0) for _ in range(sets)]
    tiles, strips, halves, sem = refs
    core = place_ref[0]

    copies = []
    for i, group, slot, row0, source, first, size in plan:
        shard = panel_refs[i]
        rows = shard.shape[-2]
        row = pl.multiple_of(place_ref[4 + row0] * rows, rows)
        at = pl.multiple_of(2 * place_ref[1 + group], 2)
        view = shard.at[:, pl.ds(source, size)] if slot is None else shard.at[slot, :, pl.ds(source, size)]
        copies.append(
            pltpu.make_async_copy(
                view, tiles.at[pl.ds(at, 2), pl.ds(first, size), :, pl.ds(row, rows), :], sem.at[len(copies)]
            )
        )
    for copy in copies:
        copy.start()
    for copy in copies:
        copy.wait()

    for k in range(sets):
        info_ref, amp_ref, out_ref = info_refs[k], amp_refs[k], out_refs[k]

        @pl.loop(0, amp_ref.shape[0])
        def _(p):
            rel = info_ref[p, 0]
            live = [info_ref[p, 1 + a] > 0 for a in range(DW)]
            masked = jnp.concatenate(
                [
                    jnp.concatenate(
                        [
                            jnp.where(live[a] & live[b], amp_ref[p, pl.ds(a * VB, VB), pl.ds(b * VB, VB)], 0)
                            for b in range(DW)
                        ],
                        axis=1,
                    )
                    for a in range(DW)
                ],
                axis=0,
            ).astype(jnp.bfloat16)
            for j in range(chunk):
                for a in range(DW):
                    d = jnp.bitwise_xor(rel + a, core)
                    strips[pl.ds(a * VB, VB), pl.ds(j * DW * VB, DW * VB)] = jnp.concatenate(
                        [tiles[d, j, b - a + DW - 1] for b in range(DW)], axis=1
                    )
            for j in range(chunk):
                cols = pl.ds(j * DW * VB, DW * VB)
                halves[:, cols] = jnp.dot(
                    strips[:, cols], masked, preferred_element_type=jnp.float32
                ).astype(jnp.bfloat16)
            ladder = lax.dot_general(
                halves[...], strips[...], (((1,), (1,)), ((), ())), preferred_element_type=jnp.float32
            )
            for a in range(DW):
                for b in range(DW):
                    at = (p, pl.ds(a * VB, VB), pl.ds(b * VB, VB))
                    part = ladder[a * VB : (a + 1) * VB, b * VB : (b + 1) * VB]
                    if has_sum:
                        part = part + sum_refs[k][at]
                    out_ref[at] = jnp.where(live[a] & live[b], part, 0.0)


def ladder(plan, chunk, place, pairs, panels, totals):
    infos, amps = zip(*pairs)
    npair, width, _ = amps[0].shape
    sets = len(pairs)
    vmem = pl.BlockSpec(memory_space=pltpu.VMEM)
    smem = pl.BlockSpec(memory_space=pltpu.SMEM)
    offs, rows, vb = panels[0].shape[-3:]
    totals = totals or []
    at = 1 + 2 * sets + len(panels)
    return pl.pallas_call(
        functools.partial(ladder_kernel, plan, chunk, sets, len(panels), bool(totals)),
        out_shape=[jax.ShapeDtypeStruct((npair, width, width), jnp.float32)] * sets,
        in_specs=[smem] * (1 + sets) + [vmem] * (sets + len(panels) + len(totals)),
        out_specs=[vmem] * sets,
        scratch_shapes=[
            pltpu.VMEM((PANELS, chunk, offs, VB, vb), jnp.bfloat16),
            pltpu.VMEM((width, chunk * width), jnp.bfloat16),
            pltpu.VMEM((width, chunk * width), jnp.bfloat16),
            pltpu.SemaphoreType.DMA((len(plan),)),
        ],
        input_output_aliases={at + k: k for k in range(len(totals))},
        compiler_params=pltpu.CompilerParams(vmem_limit_bytes=24 << 20),
        cost_estimate=pl.CostEstimate(
            flops=sets * npair * chunk * 4 * width**3, bytes_accessed=8 << 20, transcendentals=0
        ),
    )(place, *infos, *amps, *panels, *totals)


def after(x, *tokens):
    return lax.optimization_barrier((x, *tokens))[0]


def solution(mesh):
    nv, nz = mesh.shape["vblk"], mesh.shape["pair"]
    chips = nv // 2

    def moves(step):
        pairs = []
        for v in range(nv):
            for z in range(nz):
                to = step(v // 2, v % 2, z)
                if to is not None and 0 <= to[0] < chips:
                    pairs.append((v * nz + z, (to[0] * 2 + to[1]) * nz + to[2]))
        return pairs

    sideways = [moves(lambda i, c, z, s=s: (i, c, z ^ s)) for s in range(1, nz)]
    neighbour = moves(lambda i, c, z: (i ^ 1, c, z))
    relay = moves(lambda i, c, z: (i - 2 if i % 2 else i + 2, c, z))
    sibling = moves(lambda i, c, z: (i, 1 - c, z))

    def send(x, pairs, name):
        with jax.named_scope(name):
            return lax.ppermute(x, AXES, pairs)

    def local(amplitudes, domain_mask, centers, chol_panel):
        v = lax.axis_index("vblk")
        z = lax.axis_index("pair")
        core = v & 1
        odd = (v >> 1) & 1
        near = 2 - 2 * odd
        place = jnp.where(
            jnp.arange(8) < 4,
            jnp.where(
                jnp.arange(8) == 0,
                core,
                jnp.where(jnp.arange(8) == 1, 1, jnp.where(jnp.arange(8) == 2, near, 2 - near)),
            ),
            z ^ (jnp.arange(8) - 4),
        ).astype(jnp.int32)
        half = chol_panel.shape[1] // 2
        mine = lax.dynamic_slice_in_dim(chol_panel[0], core * half, half, axis=0)
        give = lax.dynamic_slice_in_dim(chol_panel[0], (1 - core) * half, half, axis=0)
        own = jnp.stack([mine, send(give, sibling, "give")])
        rel = centers - (v - core) + 1
        info = jnp.concatenate([rel[:, None], domain_mask], axis=1)
        memo = {}
        starts = [sum(CHUNKS[:j]) for j in range(len(CHUNKS))]
        first_slot = 1 if OWN_FIRST else 0

        def operand(kind, j):
            if kind == "z":
                return own[:, starts[j] : starts[j] + CHUNKS[j]]
            if kind == "x":
                return own if j == "own" else get("g", j)
            if kind == "y":
                return get("x", j)
            return {"far": amplitudes, "info": info}[j]

        def get(kind, j):
            name = f"{kind}_{j}"
            if name not in memo:
                if kind == "g":
                    part = operand("z", j)
                    memo[name] = jnp.stack(([] if OWN_FIRST else [part]) + get("z", j))
                elif kind == "k":
                    memo[name] = run(j)
                else:
                    x = operand(kind, j)
                    tokens = [t for d in DEPS.get(name, ()) for t in jax.tree.leaves(get(*spelt(d)))]
                    if tokens:
                        x = after(x, *tokens)
                    if kind == "z":
                        memo[name] = [send(x, m, name) for m in sideways]
                    else:
                        memo[name] = send(x, {"x": neighbour, "y": relay, "p": sibling}[kind], name)
            return memo[name]

        def spelt(d):
            kind, j = d.split("_")
            return kind, int(j) if j.isdigit() else j

        def run(g):
            group = KGROUPS[g]
            panels, plan, first = [], [], 0
            for j in group:
                if OWN_FIRST:
                    if j == group[0]:
                        panels += [own, get("x", "own"), get("y", "own")]
                    for i in range(3):
                        plan.append((i, i, None, 0, starts[j], first, CHUNKS[j]))
                got = [get("g", j), get("x", j), get("y", j)]
                for i in range(3):
                    for s in range(nz - first_slot):
                        plan.append((len(panels) + i, i, s, s + first_slot, 0, first, CHUNKS[j]))
                panels += got
                first += CHUNKS[j]
            pairs = [(info, amplitudes), (get("p", "info"), get("p", "far"))]
            totals = get("k", g - 1) if g else None
            if g < len(KGROUPS) - 1:
                return ladder(plan, first, place, pairs, panels, totals)
            theirs = ladder(plan, first, place, pairs[1:], panels, totals and totals[1:])
            ours = ladder(plan, first, place, pairs[:1], panels, totals and totals[:1])
            return [ours[0], theirs[0]]

        ours, theirs = get("k", len(KGROUPS) - 1)
        return ours + send(theirs, sibling, "sums")

    return jax.shard_map(
        local,
        mesh=mesh,
        in_specs=(
            P(AXES, None, None),
            P(AXES, None),
            P(AXES),
            P("vblk", None, None, "pair", None),
        ),
        out_specs=P(AXES, None, None),
        check_vma=False,
    )
```

```python
import functools

import jax
import jax.numpy as jnp
from jax import lax
from jax.experimental import pallas as pl
from jax.experimental.pallas import tpu as pltpu
from jax.sharding import PartitionSpec as P

VB = 128
DW = 3
PANELS = 6
CHUNKS = (1, 1, 1, 1)
KGROUPS = ((0,), (1,), (2,), (3,))
OWN_FIRST = True
DEPS = {'x_3': ['k_0'], 'y_3': ['k_1'], 'z_2': ['x_own']}
AXES = ("vblk", "pair")


def ladder_kernel(plan, chunk, sets, npanel, has_sum, *refs):
    refs = list(refs)
    place_ref = refs.pop(0)
    info_refs = [refs.pop(0) for _ in range(sets)]
    amp_refs = [refs.pop(0) for _ in range(sets)]
    panel_refs = [refs.pop(0) for _ in range(npanel)]
    sum_refs = [refs.pop(0) for _ in range(sets)] if has_sum else []
    out_refs = [refs.pop(0) for _ in range(sets)]
    (tiles,) = refs
    core = place_ref[0]

    for i, group, slot, row0, source, first, size in plan:
        shard = panel_refs[i]
        rows = shard.shape[-2]
        row = pl.multiple_of(place_ref[4 + row0] * rows, rows)
        at = 2 * place_ref[1 + group]
        for k in range(2):
            for j in range(size):
                piece = shard[k, source + j] if slot is None else shard[slot, k, source + j]
                tiles[at + k, first + j, :, pl.ds(row, rows), :] = piece

    for k in range(sets):
        info_ref, amp_ref, out_ref = info_refs[k], amp_refs[k], out_refs[k]

        @pl.loop(0, amp_ref.shape[0])
        def _(p):
            live = [jnp.where(info_ref[p, 1 + a] > 0, 1, 0) for a in (0, DW - 1)]
            count = live[0] + 1 + live[1]
            start = 1 - live[0]

            def blank(block):
                dead = pl.ds(pl.multiple_of(block * VB, VB), VB)
                out_ref[p, dead, :] = jnp.zeros((VB, DW * VB), jnp.float32)
                out_ref[p, :, dead] = jnp.zeros((DW * VB, VB), jnp.float32)

            for n in range(1, DW + 1):

                @pl.when(count == n)
                def _():
                    first = start if n < DW else 0
                    d = info_ref[p, 0] + first
                    here = pl.ds(pl.multiple_of(first * VB, VB), n * VB) if n < DW else slice(None)
                    amps = amp_ref[p, here, here]
                    blocks = [
                        jnp.concatenate(
                            [
                                jnp.concatenate(
                                    [tiles[jnp.bitwise_xor(d + a, core), j, b - a + DW - 1] for b in range(n)],
                                    axis=1,
                                )
                                for a in range(n)
                            ],
                            axis=0,
                        )
                        for j in range(chunk)
                    ]
                    halves = [
                        jnp.dot(x, amps, preferred_element_type=jnp.float32).astype(jnp.bfloat16) for x in blocks
                    ]
                    ladder = lax.dot_general(
                        jnp.concatenate(halves, axis=1),
                        jnp.concatenate(blocks, axis=1),
                        (((1,), (1,)), ((), ())),
                        preferred_element_type=jnp.float32,
                    )
                    if has_sum:
                        ladder = ladder + sum_refs[k][p, here, here]
                    out_ref[p, here, here] = ladder
                    if n == 1:
                        blank(0)
                        blank(DW - 1)
                    if n == 2:
                        blank(jnp.where(live[0] > 0, DW - 1, 0))


def ladder(plan, chunk, place, pairs, panels, totals):
    infos, amps = zip(*pairs)
    npair, width, _ = amps[0].shape
    sets = len(pairs)
    vmem = pl.BlockSpec(memory_space=pltpu.VMEM)
    smem = pl.BlockSpec(memory_space=pltpu.SMEM)
    offs, rows, vb = panels[0].shape[-3:]
    totals = totals or []
    at = 1 + 2 * sets + len(panels)
    return pl.pallas_call(
        functools.partial(ladder_kernel, plan, chunk, sets, len(panels), bool(totals)),
        out_shape=[jax.ShapeDtypeStruct((npair, width, width), jnp.float32)] * sets,
        in_specs=[smem] * (1 + sets) + [vmem] * (sets + len(panels) + len(totals)),
        out_specs=[vmem] * sets,
        scratch_shapes=[
            pltpu.VMEM((PANELS, chunk, offs, VB, vb), jnp.bfloat16),
        ],
        input_output_aliases={at + k: k for k in range(len(totals))},
        compiler_params=pltpu.CompilerParams(vmem_limit_bytes=16 << 20),
        cost_estimate=pl.CostEstimate(
            flops=sets * npair * chunk * 4 * width**3, bytes_accessed=8 << 20, transcendentals=0
        ),
    )(place, *infos, *amps, *panels, *totals)


def after(x, *tokens):
    return lax.optimization_barrier((x, *tokens))[0]


def solution(mesh):
    nv, nz = mesh.shape["vblk"], mesh.shape["pair"]
    chips = nv // 2

    def moves(step):
        pairs = []
        for v in range(nv):
            for z in range(nz):
                to = step(v // 2, v % 2, z)
                if to is not None and 0 <= to[0] < chips:
                    pairs.append((v * nz + z, (to[0] * 2 + to[1]) * nz + to[2]))
        return pairs

    sideways = [moves(lambda i, c, z, s=s: (i, c, z ^ s)) for s in range(1, nz)]
    neighbour = moves(lambda i, c, z: (i ^ 1, c, z))
    relay = moves(lambda i, c, z: (i - 2 if i % 2 else i + 2, c, z))
    sibling = moves(lambda i, c, z: (i, 1 - c, z))

    def send(x, pairs, name):
        with jax.named_scope(name):
            return lax.ppermute(x, AXES, pairs)

    def local(amplitudes, domain_mask, centers, chol_panel):
        v = lax.axis_index("vblk")
        z = lax.axis_index("pair")
        core = v & 1
        odd = (v >> 1) & 1
        near = 2 - 2 * odd
        place = jnp.where(
            jnp.arange(8) < 4,
            jnp.where(
                jnp.arange(8) == 0,
                core,
                jnp.where(jnp.arange(8) == 1, 1, jnp.where(jnp.arange(8) == 2, near, 2 - near)),
            ),
            z ^ (jnp.arange(8) - 4),
        ).astype(jnp.int32)
        half = chol_panel.shape[1] // 2
        mine = lax.dynamic_slice_in_dim(chol_panel[0], core * half, half, axis=0)
        give = lax.dynamic_slice_in_dim(chol_panel[0], (1 - core) * half, half, axis=0)
        own = jnp.stack([mine, send(give, sibling, "give")])
        rel = centers - (v - core) + 1
        info = jnp.concatenate([rel[:, None], domain_mask], axis=1)
        memo = {}
        starts = [sum(CHUNKS[:j]) for j in range(len(CHUNKS))]
        first_slot = 1 if OWN_FIRST else 0

        def operand(kind, j):
            if kind == "z":
                return own[:, starts[j] : starts[j] + CHUNKS[j]]
            if kind == "x":
                return own if j == "own" else get("g", j)
            if kind == "y":
                return get("x", j)
            return {"far": amplitudes, "info": info}[j]

        def get(kind, j):
            name = f"{kind}_{j}"
            if name not in memo:
                if kind == "g":
                    part = operand("z", j)
                    memo[name] = jnp.stack(([] if OWN_FIRST else [part]) + get("z", j))
                elif kind == "k":
                    memo[name] = run(j)
                else:
                    x = operand(kind, j)
                    tokens = [t for d in DEPS.get(name, ()) for t in jax.tree.leaves(get(*spelt(d)))]
                    if tokens:
                        x = after(x, *tokens)
                    if kind == "z":
                        memo[name] = [send(x, m, name) for m in sideways]
                    else:
                        memo[name] = send(x, {"x": neighbour, "y": relay, "p": sibling}[kind], name)
            return memo[name]

        def spelt(d):
            kind, j = d.split("_")
            return kind, int(j) if j.isdigit() else j

        def run(g):
            group = KGROUPS[g]
            panels, plan, first = [], [], 0
            for j in group:
                if OWN_FIRST:
                    if j == group[0]:
                        panels += [own, get("x", "own"), get("y", "own")]
                    for i in range(3):
                        plan.append((i, i, None, 0, starts[j], first, CHUNKS[j]))
                got = [get("g", j), get("x", j), get("y", j)]
                for i in range(3):
                    for s in range(nz - first_slot):
                        plan.append((len(panels) + i, i, s, s + first_slot, 0, first, CHUNKS[j]))
                panels += got
                first += CHUNKS[j]
            pairs = [(info, amplitudes), (get("p", "info"), get("p", "far"))]
            totals = get("k", g - 1) if g else None
            if g < len(KGROUPS) - 1:
                return ladder(plan, first, place, pairs, panels, totals)
            theirs = ladder(plan, first, place, pairs[1:], panels, totals and totals[1:])
            ours = ladder(plan, first, place, pairs[:1], panels, totals and totals[:1])
            return [ours[0], theirs[0]]

        ours, theirs = get("k", len(KGROUPS) - 1)
        return ours + send(theirs, sibling, "sums")

    return jax.shard_map(
        local,
        mesh=mesh,
        in_specs=(
            P(AXES, None, None),
            P(AXES, None),
            P(AXES),
            P("vblk", None, None, "pair", None),
        ),
        out_specs=P(AXES, None, None),
        check_vma=False,
    )
```

```python
import functools

import jax
import jax.numpy as jnp
from jax import lax
from jax.experimental import pallas as pl
from jax.experimental.pallas import tpu as pltpu
from jax.sharding import PartitionSpec as P

VB = 128
DW = 3
PANELS = 6
CUTS = (2, 2)
DEPS = {'x_1': ['p_1', 'x_0'], 'x_2': ['x_0', 'x_1', 'y_0'], 'x_3': ['x_1', 'y_0'], 'x_4': ['x_2', 'y_1'], 'y_3': ['y_2'], 'z_2': ['p_1'], 'z_3': ['z_1'], 'z_4': ['x_1', 'z_1']}
AXES = ("vblk", "pair")


def ladder_kernel(plan, chunk, sets, npanel, has_sum, *refs):
    refs = list(refs)
    place_ref = refs.pop(0)
    info_refs = [refs.pop(0) for _ in range(sets)]
    amp_refs = [refs.pop(0) for _ in range(sets)]
    panel_refs = [refs.pop(0) for _ in range(npanel)]
    sum_refs = [refs.pop(0) for _ in range(sets)] if has_sum else []
    out_refs = [refs.pop(0) for _ in range(sets)]
    (tiles,) = refs
    core = place_ref[0]

    for i, group, slot, row0, source, first, size in plan:
        shard = panel_refs[i]
        rows = shard.shape[-2]
        row = pl.multiple_of(place_ref[4 + row0] * rows, rows)
        at = 2 * place_ref[1 + group]
        for k in range(2):
            for j in range(size):
                piece = shard[k, source + j] if slot is None else shard[slot, k, source + j]
                tiles[at + k, first + j, :, pl.ds(row, rows), :] = piece

    for k in range(sets):
        info_ref, amp_ref, out_ref = info_refs[k], amp_refs[k], out_refs[k]

        @pl.loop(0, amp_ref.shape[0])
        def _(p):
            live = [jnp.where(info_ref[p, 1 + a] > 0, 1, 0) for a in (0, DW - 1)]
            count = live[0] + 1 + live[1]
            start = 1 - live[0]

            def blank(block):
                dead = pl.ds(pl.multiple_of(block * VB, VB), VB)
                out_ref[p, dead, :] = jnp.zeros((VB, DW * VB), out_ref.dtype)
                out_ref[p, :, dead] = jnp.zeros((DW * VB, VB), out_ref.dtype)

            for n in range(1, DW + 1):

                @pl.when(count == n)
                def _():
                    first = start if n < DW else 0
                    d = info_ref[p, 0] + first
                    here = pl.ds(pl.multiple_of(first * VB, VB), n * VB) if n < DW else slice(None)
                    amps = amp_ref[p, here, here]
                    blocks = [
                        jnp.concatenate(
                            [
                                jnp.concatenate(
                                    [tiles[jnp.bitwise_xor(d + a, core), j, b - a + DW - 1] for b in range(n)],
                                    axis=1,
                                )
                                for a in range(n)
                            ],
                            axis=0,
                        )
                        for j in range(chunk)
                    ]
                    halves = [
                        jnp.dot(x, amps, preferred_element_type=jnp.float32).astype(jnp.bfloat16) for x in blocks
                    ]
                    ladder = lax.dot_general(
                        jnp.concatenate(halves, axis=1),
                        jnp.concatenate(blocks, axis=1),
                        (((1,), (1,)), ((), ())),
                        preferred_element_type=jnp.float32,
                    )
                    if has_sum:
                        ladder = ladder + sum_refs[k][p, here, here]
                    out_ref[p, here, here] = ladder.astype(out_ref.dtype)
                    if n == 1:
                        blank(0)
                        blank(DW - 1)
                    if n == 2:
                        blank(jnp.where(live[0] > 0, DW - 1, 0))


def ladder(plan, chunk, place, pairs, panels, totals, kind=jnp.float32):
    infos, amps = zip(*pairs)
    npair, width, _ = amps[0].shape
    sets = len(pairs)
    vmem = pl.BlockSpec(memory_space=pltpu.VMEM)
    smem = pl.BlockSpec(memory_space=pltpu.SMEM)
    offs, rows, vb = panels[0].shape[-3:]
    totals = totals or []
    at = 1 + 2 * sets + len(panels)
    return pl.pallas_call(
        functools.partial(ladder_kernel, plan, chunk, sets, len(panels), bool(totals)),
        out_shape=[jax.ShapeDtypeStruct((npair, width, width), kind)] * sets,
        in_specs=[smem] * (1 + sets) + [vmem] * (sets + len(panels) + len(totals)),
        out_specs=[vmem] * sets,
        scratch_shapes=[
            pltpu.VMEM((PANELS, chunk, offs, VB, vb), jnp.bfloat16),
        ],
        input_output_aliases={at + k: k for k in range(len(totals)) if kind == totals[k].dtype},
        compiler_params=pltpu.CompilerParams(vmem_limit_bytes=16 << 20),
        cost_estimate=pl.CostEstimate(
            flops=sets * npair * chunk * 4 * width**3, bytes_accessed=8 << 20, transcendentals=0
        ),
    )(place, *infos, *amps, *panels, *totals)


def after(x, *tokens):
    return lax.optimization_barrier((x, *tokens))[0]


def solution(mesh):
    nv, nz = mesh.shape["vblk"], mesh.shape["pair"]
    chips = nv // 2

    def moves(step):
        pairs = []
        for v in range(nv):
            for z in range(nz):
                to = step(v // 2, v % 2, z)
                if to is not None and 0 <= to[0] < chips:
                    pairs.append((v * nz + z, (to[0] * 2 + to[1]) * nz + to[2]))
        return pairs

    sideways = [moves(lambda i, c, z, s=s: (i, c, z ^ s)) for s in range(1, nz)]
    neighbour = moves(lambda i, c, z: (i ^ 1, c, z))
    relay = moves(lambda i, c, z: (i - 2 if i % 2 else i + 2, c, z))
    sibling = moves(lambda i, c, z: (i, 1 - c, z))

    def send(x, pairs, name):
        with jax.named_scope(name):
            return lax.ppermute(x, AXES, pairs)

    def local(amplitudes, domain_mask, centers, chol_panel):
        v = lax.axis_index("vblk")
        z = lax.axis_index("pair")
        core = v & 1
        odd = (v >> 1) & 1
        near = 2 - 2 * odd
        place = jnp.where(
            jnp.arange(8) < 4,
            jnp.where(
                jnp.arange(8) == 0,
                core,
                jnp.where(jnp.arange(8) == 1, 1, jnp.where(jnp.arange(8) == 2, near, 2 - near)),
            ),
            z ^ (jnp.arange(8) - 4),
        ).astype(jnp.int32)
        half = chol_panel.shape[1] // 2
        mine = lax.dynamic_slice_in_dim(chol_panel[0], core * half, half, axis=0)
        give = lax.dynamic_slice_in_dim(chol_panel[0], (1 - core) * half, half, axis=0)
        own = jnp.stack([mine, send(give, sibling, "give")])
        rel = centers - (v - core) + 1
        info = jnp.concatenate([rel[:, None], domain_mask], axis=1)
        memo = {}
        whole = nz - 1
        firsts = [sum(CUTS[:k]) for k in range(len(CUTS))]

        def operand(kind, j):
            if kind == "z":
                return own if j < whole else own[:, firsts[j - whole] : firsts[j - whole] + CUTS[j - whole]]
            if kind == "x":
                return get("z", j) if j else own
            if kind == "y":
                return get("x", j)
            return after(info if j else amplitudes, own)

        def get(kind, j):
            name = f"{kind}_{j}"
            if name not in memo:
                if kind == "k":
                    memo[name] = run(j)
                else:
                    x = operand(kind, j)
                    tokens = [t for d in DEPS.get(name, ()) for t in jax.tree.leaves(get(d[0], int(d[2:])))]
                    if tokens:
                        x = after(x, *tokens)
                    pairs = {"x": neighbour, "y": relay, "p": sibling}.get(kind) or sideways[min(j, whole) - 1]
                    memo[name] = send(x, pairs, name)
            return memo[name]

        def run(g):
            panels, plan = [], []
            for j in [*range(whole), whole + g]:
                for i, x in enumerate((get("z", j) if j else own, get("x", j), get("y", j))):
                    source = firsts[g] if j < whole else 0
                    plan.append((len(panels), i, None, min(j, whole), source, 0, CUTS[g]))
                    panels.append(x)
            pairs = [(info, amplitudes), (get("p", 1), get("p", 0))]
            totals = get("k", g - 1) if g else None
            if g < len(CUTS) - 1:
                return ladder(plan, CUTS[g], place, pairs, panels, totals)
            theirs = ladder(plan, CUTS[g], place, pairs[1:], panels, totals and totals[1:], jnp.bfloat16)
            ours = ladder(plan, CUTS[g], place, pairs[:1], panels, totals and totals[:1])
            return [ours[0], theirs[0]]

        ours, theirs = get("k", len(CUTS) - 1)
        return ours + send(theirs, sibling, "sums")

    return jax.shard_map(
        local,
        mesh=mesh,
        in_specs=(
            P(AXES, None, None),
            P(AXES, None),
            P(AXES),
            P("vblk", None, None, "pair", None),
        ),
        out_specs=P(AXES, None, None),
        check_vma=False,
    )
```

```python
import functools

import jax
import jax.numpy as jnp
from jax import lax
from jax.experimental import pallas as pl
from jax.experimental.pallas import tpu as pltpu
from jax.sharding import PartitionSpec as P

VB = 128
DW = 3
PANELS = 6
CUTS = (2, 2)
DEPS = {'x_1': ['p_1', 'x_0'], 'x_2': ['x_0', 'x_1'], 'x_3': ['x_1', 'y_0'], 'x_4': ['x_2', 'y_1'], 'y_3': ['y_2'], 'z_2': ['p_1'], 'z_3': ['x_0'], 'z_4': ['x_0', 'z_1']}
AXES = ("vblk", "pair")


def ladder_kernel(plan, chunk, sets, npanel, has_sum, *refs):
    refs = list(refs)
    place_ref = refs.pop(0)
    info_refs = [refs.pop(0) for _ in range(sets)]
    amp_refs = [refs.pop(0) for _ in range(sets)]
    panel_refs = [refs.pop(0) for _ in range(npanel)]
    sum_refs = [refs.pop(0) for _ in range(sets)] if has_sum else []
    out_refs = [refs.pop(0) for _ in range(sets)]
    (tiles,) = refs
    core = place_ref[0]

    for i, group, slot, row0, source, first, size in plan:
        shard = panel_refs[i]
        rows = shard.shape[-2]
        row = pl.multiple_of(place_ref[4 + row0] * rows, rows)
        at = 2 * place_ref[1 + group]
        for k in range(2):
            for j in range(size):
                piece = shard[k, source + j] if slot is None else shard[slot, k, source + j]
                tiles[at + k, first + j, :, pl.ds(row, rows), :] = piece

    for k in range(sets):
        info_ref, amp_ref, out_ref = info_refs[k], amp_refs[k], out_refs[k]

        @pl.loop(0, amp_ref.shape[0])
        def _(p):
            live = [jnp.where(info_ref[p, 1 + a] > 0, 1, 0) for a in (0, DW - 1)]
            count = live[0] + 1 + live[1]
            start = 1 - live[0]

            def blank(block):
                dead = pl.ds(pl.multiple_of(block * VB, VB), VB)
                out_ref[p, dead, :] = jnp.zeros((VB, DW * VB), out_ref.dtype)
                out_ref[p, :, dead] = jnp.zeros((DW * VB, VB), out_ref.dtype)

            for n in range(1, DW + 1):

                @pl.when(count == n)
                def _():
                    first = start if n < DW else 0
                    d = info_ref[p, 0] + first
                    here = pl.ds(pl.multiple_of(first * VB, VB), n * VB) if n < DW else slice(None)
                    amps = amp_ref[p, here, here]
                    blocks = [
                        jnp.concatenate(
                            [
                                jnp.concatenate(
                                    [tiles[jnp.bitwise_xor(d + a, core), j, b - a + DW - 1] for b in range(n)],
                                    axis=1,
                                )
                                for a in range(n)
                            ],
                            axis=0,
                        )
                        for j in range(chunk)
                    ]
                    halves = [
                        jnp.dot(x, amps, preferred_element_type=jnp.float32).astype(jnp.bfloat16) for x in blocks
                    ]
                    ladder = lax.dot_general(
                        jnp.concatenate(halves, axis=1),
                        jnp.concatenate(blocks, axis=1),
                        (((1,), (1,)), ((), ())),
                        preferred_element_type=jnp.float32,
                    )
                    if has_sum:
                        ladder = ladder + sum_refs[k][p, here, here]
                    out_ref[p, here, here] = ladder.astype(out_ref.dtype)
                    if n == 1:
                        blank(0)
                        blank(DW - 1)
                    if n == 2:
                        blank(jnp.where(live[0] > 0, DW - 1, 0))


def ladder(plan, chunk, place, pairs, panels, totals, kind=jnp.float32):
    infos, amps = zip(*pairs)
    npair, width, _ = amps[0].shape
    sets = len(pairs)
    vmem = pl.BlockSpec(memory_space=pltpu.VMEM)
    smem = pl.BlockSpec(memory_space=pltpu.SMEM)
    offs, rows, vb = panels[0].shape[-3:]
    totals = totals or []
    at = 1 + 2 * sets + len(panels)
    return pl.pallas_call(
        functools.partial(ladder_kernel, plan, chunk, sets, len(panels), bool(totals)),
        out_shape=[jax.ShapeDtypeStruct((npair, width, width), kind)] * sets,
        in_specs=[smem] * (1 + sets) + [vmem] * (sets + len(panels) + len(totals)),
        out_specs=[vmem] * sets,
        scratch_shapes=[
            pltpu.VMEM((PANELS, chunk, offs, VB, vb), jnp.bfloat16),
        ],
        input_output_aliases={at + k: k for k in range(len(totals)) if kind == totals[k].dtype},
        compiler_params=pltpu.CompilerParams(vmem_limit_bytes=16 << 20),
        cost_estimate=pl.CostEstimate(
            flops=sets * npair * chunk * 4 * width**3, bytes_accessed=8 << 20, transcendentals=0
        ),
    )(place, *infos, *amps, *panels, *totals)


def after(x, *tokens):
    return lax.optimization_barrier((x, *tokens))[0]


def solution(mesh):
    nv, nz = mesh.shape["vblk"], mesh.shape["pair"]
    chips = nv // 2

    def moves(step):
        pairs = []
        for v in range(nv):
            for z in range(nz):
                to = step(v // 2, v % 2, z)
                if to is not None and 0 <= to[0] < chips:
                    pairs.append((v * nz + z, (to[0] * 2 + to[1]) * nz + to[2]))
        return pairs

    sideways = [moves(lambda i, c, z, s=s: (i, c, z ^ s)) for s in range(1, nz)]
    neighbour = moves(lambda i, c, z: (i ^ 1, c, z))
    relay = moves(lambda i, c, z: (i - 2 if i % 2 else i + 2, c, z))
    sibling = moves(lambda i, c, z: (i, 1 - c, z))

    def send(x, pairs, name):
        with jax.named_scope(name):
            return lax.ppermute(x, AXES, pairs)

    def local(amplitudes, domain_mask, centers, chol_panel):
        v = lax.axis_index("vblk")
        z = lax.axis_index("pair")
        core = v & 1
        odd = (v >> 1) & 1
        near = 2 - 2 * odd
        place = jnp.where(
            jnp.arange(8) < 4,
            jnp.where(
                jnp.arange(8) == 0,
                core,
                jnp.where(jnp.arange(8) == 1, 1, jnp.where(jnp.arange(8) == 2, near, 2 - near)),
            ),
            z ^ (jnp.arange(8) - 4),
        ).astype(jnp.int32)
        half = chol_panel.shape[1] // 2
        mine = lax.dynamic_slice_in_dim(chol_panel[0], core * half, half, axis=0)
        give = lax.dynamic_slice_in_dim(chol_panel[0], (1 - core) * half, half, axis=0)
        own = jnp.stack([mine, send(give, sibling, "give")])
        rel = centers - (v - core) + 1
        info = jnp.concatenate([rel[:, None], domain_mask], axis=1)
        memo = {}
        whole = nz - 1
        firsts = [sum(CUTS[:k]) for k in range(len(CUTS))]

        def operand(kind, j):
            if kind == "z":
                return own if j < whole else own[:, firsts[j - whole] : firsts[j - whole] + CUTS[j - whole]]
            if kind == "x":
                return get("z", j) if j else own
            if kind == "y":
                return get("x", j)
            return after(info if j else amplitudes, own)

        def get(kind, j):
            name = f"{kind}_{j}"
            if name not in memo:
                if kind == "k":
                    memo[name] = run(j)
                else:
                    x = operand(kind, j)
                    tokens = [t for d in DEPS.get(name, ()) for t in jax.tree.leaves(get(d[0], int(d[2:])))]
                    if tokens:
                        x = after(x, *tokens)
                    pairs = {"x": neighbour, "y": relay, "p": sibling}.get(kind) or sideways[min(j, whole) - 1]
                    memo[name] = send(x, pairs, name)
            return memo[name]

        def run(g):
            panels, plan = [], []
            for j in [*range(whole), whole + g]:
                for i, x in enumerate((get("z", j) if j else own, get("x", j), get("y", j))):
                    source = firsts[g] if j < whole else 0
                    plan.append((len(panels), i, None, min(j, whole), source, 0, CUTS[g]))
                    panels.append(x)
            pairs = [(info, amplitudes), (get("p", 1), get("p", 0))]
            totals = get("k", g - 1) if g else None
            if g < len(CUTS) - 1:
                return ladder(plan, CUTS[g], place, pairs, panels, totals)
            theirs = ladder(plan, CUTS[g], place, pairs[1:], panels, totals and totals[1:], jnp.bfloat16)
            ours = ladder(plan, CUTS[g], place, pairs[:1], panels, totals and totals[:1])
            return [ours[0], theirs[0]]

        ours, theirs = get("k", len(CUTS) - 1)
        return ours + send(theirs, sibling, "sums")

    return jax.shard_map(
        local,
        mesh=mesh,
        in_specs=(
            P(AXES, None, None),
            P(AXES, None),
            P(AXES),
            P("vblk", None, None, "pair", None),
        ),
        out_specs=P(AXES, None, None),
        check_vma=False,
    )
```
